32 devices in a mesh: dp: 8 (over z, core), mp: 4 (over y, x).
Axes of the slice: x: 2, y: 2, z: 4, core: 2. Of those that a mesh axis runs over, the one named last changes fastest.
Arguments:
- student_in: bfloat16 [128, 6144], P(None, 'mp'), may hold values from -6 to 6
- teacher_hidden: bfloat16 [8192, 128], P('dp'), may hold values from -6 to 6
- w_up: bfloat16 [24576, 6144], P('dp', 'mp'), may hold values from -0.078125 to 0.078125
- w_down: bfloat16 [24576, 6144], P('dp', 'mp'), may hold values from -0.0390625 to 0.0390625
- w_proj: bfloat16 [8192, 6144], P('dp', 'mp'), may hold values from -0.0625 to 0.0625
Outputs:
- grad_up: float32 [24576, 6144], P('dp', 'mp')
- grad_down: float32 [24576, 6144], P('dp', 'mp')
- grad_proj: float32 [8192, 6144], P('dp', 'mp')
The draws below stay inside these ranges and needn't reach their ends.
All inputs are finite; a program needn't handle non-finite values.
Results may differ from the reference program's by a relative error of at most 0.005.
Values may be sent and summed in bfloat16 or wider, within the bound.
No kernel may reach another device: no remote copies, remote signals or barrier semaphores. Data moves between devices by JAX's collectives and lax.ppermute only.
A program may use at most 128 MiB of HBM per device.

```python
import math
import jax
import jax.numpy as jnp

D = 6144
FF = 24576
TD = 8192
TOKENS = 128


def shard_levels(stream_key, dims, shards, least, high):
    factor_of, own = 1.0, jax.random.fold_in(stream_key, 6)
    for axis_at, parts in shards:
        steps = jnp.exp(jax.random.uniform(jax.random.fold_in(own, axis_at), (parts,), jnp.float32, least / len(shards), high / len(shards)))
        factor_of = factor_of * jnp.repeat(steps, dims[axis_at] // parts).reshape([-1 if axis == axis_at else 1 for axis in range(len(dims))])
    return factor_of


def bell_draw(stream_key, dims, width, limit, pieces=(), dtype=jnp.bfloat16):
    loudness = shard_levels(stream_key, dims, pieces, -0.22, 0.18) if pieces else 1.0
    values = jax.random.normal(stream_key, dims, jnp.float32) * width * loudness
    return jnp.minimum(jnp.maximum(values, -limit), limit).astype(dtype)


def setup_inputs(seed: int = 0) -> dict:
    arg_keys = jax.random.split(jax.random.key(seed), 6)
    student_in = bell_draw(arg_keys[0], (TOKENS, D), 1.0, 6.0, ((1, 4),))
    teacher_hidden = bell_draw(arg_keys[1], (TD, TOKENS), 1.0, 6.0, ((0, 8),))
    w_up = bell_draw(arg_keys[2], (FF, D), D ** -0.5, 0.078125, ((0, 8), (1, 4)))
    w_down = bell_draw(arg_keys[3], (FF, D), FF ** -0.5, 0.0390625, ((0, 8), (1, 4)))
    w_proj = bell_draw(arg_keys[4], (TD, D), TD ** -0.5, 0.0625, ((0, 8), (1, 4)))
    return {"student_in": student_in, "teacher_hidden": teacher_hidden, "w_up": w_up, "w_down": w_down, "w_proj": w_proj}


def reference(student_in, teacher_hidden, w_up, w_down, w_proj):
    pre = jnp.dot(w_up, student_in.T, preferred_element_type=jnp.float32)
    active = jnp.maximum(pre, 0.0)
    hidden = (active * active).astype(jnp.bfloat16)
    student_out = jnp.dot(hidden.T, w_down, preferred_element_type=jnp.float32)
    target = jnp.dot(teacher_hidden.T, w_proj, preferred_element_type=jnp.float32)
    residual = student_out - target
    d_out = (residual * (1.0 / math.sqrt(TOKENS))).astype(jnp.bfloat16)
    grad_down = jnp.dot(hidden, d_out, preferred_element_type=jnp.float32)
    grad_proj = -jnp.dot(teacher_hidden, d_out, preferred_element_type=jnp.float32)
    d_hidden = jnp.dot(w_down, d_out.T, preferred_element_type=jnp.float32)
    d_pre = (d_hidden * (2.0 * active)).astype(jnp.bfloat16)
    grad_up = jnp.dot(d_pre, student_in, preferred_element_type=jnp.float32)
    return (grad_up, grad_down, grad_proj)
```

```python
import functools
import math

import jax
import jax.numpy as jnp
from jax import lax
from jax.experimental import pallas as pl
from jax.experimental.pallas import tpu as pltpu
from jax.sharding import PartitionSpec as P

F32, BF16 = jnp.float32, jnp.bfloat16
BOTH_LAST = (((1,), (1,)), ((), ()))
BOTH_FIRST = (((0,), (0,)), ((), ()))
PLAIN = (((1,), (0,)), ((), ()))
ANY = pl.BlockSpec(memory_space=pl.ANY)
VMEM = pl.BlockSpec(memory_space=pltpu.VMEM)
MIB = 1 << 20


def mm(left, right, dims):
    return lax.dot_general(left, right, dims, preferred_element_type=F32)


def call(kernel, outs, out_specs, in_specs, scratch, args, flops, nbytes, aliases=None, limit=28):
    return pl.pallas_call(
        kernel,
        out_shape=outs,
        in_specs=in_specs,
        out_specs=out_specs,
        scratch_shapes=scratch,
        input_output_aliases=aliases or {},
        cost_estimate=pl.CostEstimate(flops=flops, bytes_accessed=nbytes, transcendentals=0),
        compiler_params=pltpu.CompilerParams(vmem_limit_bytes=limit * MIB),
    )(*args)


def rows_of(block, size):
    return pl.multiple_of((lax.axis_index("mp") ^ block) * size, size)


def load_ahead(copies, use, depth=2):
    for copy in copies[:depth]:
        copy.start()
    for at, copy in enumerate(copies):
        copy.wait()
        use(at)
        if at + depth < len(copies):
            copies[at + depth].start()


def rows_kernel(blocks, size, parts, w, s, *refs):
    outs, (buf, sem) = refs[: len(blocks)], refs[len(blocks):]
    step = size // parts
    copies = []
    for i, block in enumerate(blocks):
        base = rows_of(block, size)
        for p in range(parts):
            at = i * parts + p
            copies.append(pltpu.make_async_copy(
                w.at[pl.ds(base + p * step, step)], buf.at[at], sem.at[at]))

    def use(at):
        out = outs[at // parts]
        out[pl.ds((at % parts) * step, step)] = mm(buf[at], s[...], BOTH_LAST).astype(out.dtype)

    load_ahead(copies, use)


def rows_times(w, s, blocks, size, dtypes, parts=2):
    k, tokens = w.shape[1], s.shape[0]
    n = len(blocks)
    return call(
        functools.partial(rows_kernel, blocks, size, parts),
        [jax.ShapeDtypeStruct((size, tokens), dt) for dt in dtypes], [VMEM] * n, [ANY, VMEM],
        [pltpu.VMEM((n * parts, size // parts, k), w.dtype), pltpu.SemaphoreType.DMA((n * parts,))],
        (w, s), 2 * n * size * k * tokens, 2 * n * size * k)


def target_kernel(parts, t, w, out, buf, sem):
    step = w.shape[0] // parts
    copies = [pltpu.make_async_copy(w.at[pl.ds(p * step, step)], buf.at[p], sem.at[p]) for p in range(parts)]

    def use(p):
        term = mm(t[pl.ds(p * step, step)], buf[p], BOTH_FIRST)
        if p == 0:
            out[...] = -term
        else:
            out[...] -= term

    load_ahead(copies, use)


def minus_target(t, w, parts=2):
    (td, k), tokens = w.shape, t.shape[1]
    return call(
        functools.partial(target_kernel, parts), jax.ShapeDtypeStruct((tokens, k), F32), VMEM, [VMEM, ANY],
        [pltpu.VMEM((parts, td // parts, k), w.dtype), pltpu.SemaphoreType.DMA((parts,))],
        (t, w), 2 * td * k * tokens, 2 * td * k)


def student_kernel(blocks, size, split, acc, w, *refs):
    n = len(blocks)
    hid, refs = refs[:n], refs[n:]
    if split:
        send, keep, buf, sem, total = refs
    else:
        total, buf, sem = refs
    copies = [pltpu.make_async_copy(w.at[pl.ds(rows_of(b, size), size)], buf.at[i], sem.at[i])
              for i, b in enumerate(blocks)]

    def use(i):
        total[...] = (acc[...] if i == 0 else total[...]) + mm(hid[i][...], buf[i], BOTH_FIRST)

    load_ahead(copies, use)
    if split:
        half = total.shape[0] // 2
        core = lax.axis_index("dp") % 2
        keep[...] = total[pl.ds(pl.multiple_of(core * half, half), half)]
        send[...] = total[pl.ds(pl.multiple_of((1 - core) * half, half), half)].astype(send.dtype)


def student(acc, w, hid, blocks, size, split=False, send_dtype=BF16):
    (tokens, k), n = acc.shape, len(blocks)
    scratch = [pltpu.VMEM((n, size, k), w.dtype), pltpu.SemaphoreType.DMA((n,))]
    if split:
        outs = [jax.ShapeDtypeStruct((tokens // 2, k), send_dtype), jax.ShapeDtypeStruct((tokens // 2, k), F32)]
        scratch.append(pltpu.VMEM((tokens, k), F32))
    else:
        outs = [jax.ShapeDtypeStruct((tokens, k), F32)]
    return call(
        functools.partial(student_kernel, blocks, size, split), outs, [VMEM] * len(outs),
        [VMEM, ANY] + [VMEM] * n, scratch, (acc, w, *hid), 2 * n * size * k * tokens, 2 * n * size * k)


def fold_kernel(nz, keep, got, own, *sends):
    rows = own.shape[0]
    z = lax.axis_index("dp") // 2
    for r in range(nz):
        at = pl.ds(pl.multiple_of((z ^ r) * rows, rows), rows)
        total = keep[at] + got[at].astype(F32)
        if r == 0:
            own[...] = total
        else:
            sends[r - 1][...] = total.astype(sends[r - 1].dtype)


def fold(keep, got, nz, send_dtype=BF16):
    half, k = keep.shape
    rows = half // nz
    return call(
        functools.partial(fold_kernel, nz),
        [jax.ShapeDtypeStruct((rows, k), F32)] + [jax.ShapeDtypeStruct((rows, k), send_dtype)] * (nz - 1),
        [VMEM] * nz, [VMEM, VMEM], [], (keep, got), half * k, 8 * half * k)


def join_kernel(nz, own, *refs):
    half = refs[nz - 1]
    out = refs[nz]
    rows = own.shape[0]
    z, core = lax.axis_index("dp") // 2, lax.axis_index("dp") % 2
    size = half.shape[0]
    for r in range(nz):
        piece = own if r == 0 else refs[r - 1]
        out[pl.ds(pl.multiple_of(core * size + (z ^ r) * rows, rows), rows)] = piece[...]
        out[pl.ds(pl.multiple_of((1 - core) * size + (z ^ r) * rows, rows), rows)] = half[pl.ds(r * rows, rows)]


def join(pieces, half):
    nz = len(pieces)
    size, k = half.shape
    return call(
        functools.partial(join_kernel, nz), jax.ShapeDtypeStruct((2 * size, k), half.dtype),
        VMEM, [VMEM] * (nz + 1), [], (*pieces, half), 0, 8 * size * k)


def largest_step(total, limit):
    return max(d for d in range(16, limit + 1, 16) if total % d == 0)


def outer_kernel(blocks, size, parts, extra, *refs):
    n = len(blocks)
    left, refs = refs[:n], refs[n:]
    right, refs = refs[0], refs[1:]
    if extra == "teacher":
        teacher, out, proj, buf, sem = refs
    elif extra == "alias":
        _, out, buf, sem = refs
    else:
        out, buf, sem = refs
    step = size // parts
    slots = buf.shape[0]
    jobs = [(left[i], p * step, step, out, rows_of(b, size) + p * step, False)
            for i, b in enumerate(blocks) for p in range(parts)]
    if extra == "teacher":
        total = proj.shape[0]
        short = largest_step(total, step)
        jobs += [(teacher, p, short, proj, p, True) for p in range(0, total, short)]
    copies = []
    for at, (src, start, count, dst, row, minus) in enumerate(jobs):
        slot = at % slots
        if at >= slots:
            copies[at - slots].wait()
        term = mm(src[pl.ds(start, count)], right[...], PLAIN)
        buf[slot, pl.ds(0, count)] = -term if minus else term
        copies.append(pltpu.make_async_copy(
            buf.at[slot, pl.ds(0, count)], dst.at[pl.ds(row, count)], sem.at[slot]))
        copies[at].start()
    for copy in copies[max(0, len(jobs) - slots):]:
        copy.wait()


def outer(left, right, blocks, size, rows, teacher=None, into=None, parts=2, slots=4):
    k, n = right.shape[1], len(blocks)
    step = size // parts
    outs = [jax.ShapeDtypeStruct((rows, k), F32)]
    args, aliases, extra, done = [*left, right], {}, "", n * size
    specs = [VMEM] * (n + 1)
    if teacher is not None:
        extra = "teacher"
        outs.append(jax.ShapeDtypeStruct((teacher.shape[0], k), F32))
        args.append(teacher)
        specs.append(VMEM)
        done += teacher.shape[0]
    elif into is not None:
        extra = "alias"
        aliases = {len(args): 0}
        args.append(into)
        specs.append(ANY)
    slots = min(slots, done // step)
    return call(
        functools.partial(outer_kernel, blocks, size, parts, extra), outs, [ANY] * len(outs), specs,
        [pltpu.VMEM((slots, step, k), F32), pltpu.SemaphoreType.DMA((slots,))],
        args, 2 * done * k * right.shape[0], 4 * done * k, aliases)


def fast_body(n_mp, n_dp, student_in, teacher_hidden, w_up, w_down, w_proj):
    tokens = student_in.shape[0]
    rows = w_up.shape[0]
    size = rows // n_mp
    nz = n_dp // 2
    others = list(range(n_mp - 1, 0, -1))

    def to(x, axis, n, r):
        return lax.ppermute(x, axis, [(i, i ^ r) for i in range(n)])

    def mp(x, r):
        return to(x, "mp", n_mp, r)

    def reduce_blocks(w, s):
        got = {}
        first, *rest = others
        (x,) = rows_times(w, s, [first], size, [BF16])
        got[first] = mp(x, first)
        if rest:
            for r, x in zip(rest, rows_times(w, s, rest, size, [BF16] * len(rest))):
                got[r] = mp(x, r)
        (own,) = rows_times(w, s, [0], size, [F32])
        return own, got

    def spread(x):
        return [x] + [mp(x, r) for r in range(1, n_mp)]

    own, got = reduce_blocks(w_up, student_in)
    acc = minus_target(teacher_hidden, w_proj)
    pre = own
    for r in sorted(got):
        pre = pre + got[r].astype(F32)
    active = jnp.maximum(pre, 0.0)
    hidden = spread((active * active).astype(BF16))
    (acc,) = student(acc, w_down, hidden[:1], [0], size)
    if n_mp > 2:
        (acc,) = student(acc, w_down, hidden[1:-1], list(range(1, n_mp - 1)), size)
    send, keep = student(acc, w_down, hidden[-1:], [n_mp - 1], size, split=True)
    half = to(send, "dp", n_dp, 1)
    own, *sends = fold(keep, half, nz)
    residual = own
    for r in range(1, nz):
        residual = residual + to(sends[r - 1], "dp", n_dp, 2 * r).astype(F32)
    d_local = (residual * (1.0 / math.sqrt(tokens))).astype(BF16)
    pieces = [d_local] + [to(d_local, "dp", n_dp, 2 * r) for r in range(1, nz)]
    d_out = join(pieces, to(jnp.concatenate(pieces, 0), "dp", n_dp, 1))

    own, got = reduce_blocks(w_down, d_out)
    grad_down, grad_proj = outer(hidden, d_out, list(range(n_mp)), size, rows, teacher=teacher_hidden)
    d_hidden = own
    for r in sorted(got):
        d_hidden = d_hidden + got[r].astype(F32)
    d_pre = spread((d_hidden * (2.0 * active)).astype(BF16))
    (grad_up,) = outer(d_pre[:1], student_in, [0], size, rows)
    if n_mp > 2:
        (grad_up,) = outer(d_pre[1:-1], student_in, list(range(1, n_mp - 1)), size, rows, into=grad_up)
    (grad_up,) = outer(d_pre[-1:], student_in, [n_mp - 1], size, rows, into=grad_up)
    return grad_up, grad_down, grad_proj


def plain_body(student_in, teacher_hidden, w_up, w_down, w_proj):
    tokens = student_in.shape[0]
    pre = lax.psum(mm(w_up, student_in, BOTH_LAST), "mp")
    active = jnp.maximum(pre, 0.0)
    hidden = (active * active).astype(BF16)
    part = mm(hidden, w_down, BOTH_FIRST) - mm(teacher_hidden, w_proj, BOTH_FIRST)
    residual = lax.psum_scatter(part, "dp", scatter_dimension=0, tiled=True)
    d_local = (residual * (1.0 / math.sqrt(tokens))).astype(BF16)
    d_out = lax.all_gather(d_local, "dp", axis=0, tiled=True)
    grad_down = mm(hidden, d_out, PLAIN)
    grad_proj = -mm(teacher_hidden, d_out, PLAIN)
    d_hidden = lax.psum(mm(w_down, d_out, BOTH_LAST), "mp")
    d_pre = (d_hidden * (2.0 * active)).astype(BF16)
    grad_up = mm(d_pre, student_in, PLAIN)
    return grad_up, grad_down, grad_proj


def solution(mesh):
    n_mp, n_dp = mesh.shape["mp"], mesh.shape["dp"]

    def body(student_in, teacher_hidden, w_up, w_down, w_proj):
        tokens, size = student_in.shape[0], w_up.shape[0] // n_mp
        fits = (
            n_mp in (2, 4, 8) and n_dp in (2, 4, 8, 16)
            and w_up.shape[0] % n_mp == 0 and size % 64 == 0
            and tokens % (16 * n_dp) == 0 and student_in.shape[1] % 128 == 0
            and teacher_hidden.shape[0] % 32 == 0
        )
        args = (student_in, teacher_hidden, w_up, w_down, w_proj)
        return fast_body(n_mp, n_dp, *args) if fits else plain_body(*args)

    return jax.shard_map(
        body,
        mesh=mesh,
        in_specs=(P(None, "mp"), P("dp", None), P("dp", "mp"), P("dp", "mp"), P("dp", "mp")),
        out_specs=(P("dp", "mp"), P("dp", "mp"), P("dp", "mp")),
        check_vma=False,
    )
```
